256 devices in a mesh: occ: 64 (over z, y, core), ao: 4 (over x).
Axes of the slice: x: 4, y: 4, z: 8, core: 2. Of those that a mesh axis runs over, the one named last changes fastest.
Arguments:
- amplitudes: bfloat16 [256, 256, 256], P('occ', None, 'ao'), may hold values from -6 to 6
- orbitals: bfloat16 [512, 256], replicated, may hold values from -0.375 to 0.375
- tiles: bfloat16 [4096, 512, 512], P('occ', None, 'ao'), may hold values from -0.125 to 0.125
- tile_count: int32 [64], replicated, may hold values from 1 to 64, 2048 in all
- tile_row: int32 [4096], replicated, may hold values from 0 to 7
- tile_src: int32 [4096, 1], replicated, may hold values from 0 to 63; in each aligned block of 64 rows (0 to 63, 64 to 127, ...) at most 2 rows name the same one
- tile_sub: int32 [4096], replicated, may hold values from 0 to 7
Outputs:
- sigma_out: bfloat16 [256, 256, 256], P('occ', None, 'ao')
The draws below stay inside these ranges and needn't reach their ends.
Inputs may be any that keep to these rules, and one draw needn't show every extreme that they name: `tile_count`: each occ index owns between 1 and 64 live slots, the first ones of its 64 slots; some index owns exactly 64. `tile_src`: among the 64 slots of one owner no source index is named more than 2 times, and some owner names one source exactly 2 times.
All inputs are finite; a program needn't handle non-finite values.
Results may differ from the reference program's by a relative error of at most 0.024.
Values may be sent and summed in bfloat16 or wider, within the bound.
A program may use at most 128 MiB of HBM per device.

```python
import math
import jax
import jax.numpy as jnp
import numpy as np
from jax import lax

NOCC = 256
NVIR = 256
NAO = 512
CAP = 64
TILE_SLOTS = 4096
TILES = 2048
ROWBLK = 8
QMAX = 2
N_OCC = 64


def touch_ends(values, key, smallest, high):
    place = [jax.random.randint(jax.random.fold_in(key, axis), (), 0, length) for axis, length in enumerate(values.shape)]
    widest = values.shape.index(max(values.shape))
    neighbour = place[:widest] + [(place[widest] + 1) % values.shape[widest]] + place[widest + 1:]
    return values.at[tuple(place)].set(smallest).at[tuple(neighbour)].set(high)


def block_levels(own_key, shape, pieces, low, high):
    def one(axis_at, parts):
        steps = jax.random.uniform(jax.random.fold_in(jax.random.fold_in(own_key, 6), axis_at), (parts,), jnp.float32, low / len(pieces), high / len(pieces))
        return jnp.repeat(jnp.exp(steps), shape[axis_at] // parts).reshape((-1,) + (1,) * (len(shape) - axis_at - 1))

    gain = one(*pieces[0])
    for cut in pieces[1:]:
        gain = gain * one(*cut)
    return gain


def length_profile(number_of, total, most, slope):
    weights = [(1 << 20) // math.isqrt(grade ** slope) + 1 for grade in range(2, number_of + 1)]
    surplus, counts = total - most - (number_of - 1), [1] * (number_of - 1)
    while surplus > 0:
        candidates = [i for i in range(number_of - 1) if counts[i] < most]
        whole, left = sum([weights[i] for i in candidates]), surplus
        for i in candidates:
            addition = min(most - counts[i], max(1, left * weights[i] // whole), surplus)
            counts[i] = counts[i] + addition
            surplus = surplus - addition
    return np.array([most] + counts)


def uneven(key, count, total, limit, lean):
    if count == 2:
        one = jax.random.randint(key, (), max(1, total - limit), min(limit, total - 1) + 1)
        return jnp.stack([one, total - one])
    sizes = jnp.asarray(length_profile(count, total, limit, lean), jnp.int32)
    couples = (count - 1) // 2
    source_of, taker = sizes[1:1 + 2 * couples:2], sizes[2:2 + 2 * couples:2]
    room = jnp.minimum(source_of - 1, limit - taker)
    shifted = jax.random.randint(jax.random.fold_in(key, 1), (couples,), 0, 1 << 20) % (room + 1)
    sizes = sizes.at[1:1 + 2 * couples:2].set(source_of - shifted).at[2:2 + 2 * couples:2].set(taker + shifted)
    return sizes[jax.random.permutation(jax.random.fold_in(key, 2), count)]


def routed_block(stream_key, own, number, rows, count, top, reach, lean):
    order = jax.random.permutation(stream_key, count)
    crowded, common = portions_of(count, rows * top, reach, lean, True), portions_of(count, rows * top, reach, lean, False)
    places = jnp.arange(count)

    def named(sizes, offset_by):
        used = int((sizes > 0).sum())
        fixed = max(1, used // 4)
        shifted = fixed + (places - fixed + offset_by * (used - fixed)) % max(1, count - fixed)
        return jnp.zeros((count,), jnp.int32).at[order[jnp.where(places < fixed, places, shifted)]].set(jnp.asarray(sizes, jnp.int32))

    sizes = jnp.where(number % 4 == 0, named(crowded, number // 4), named(common, number - number // 4 - 1))
    mixed = jax.random.permutation(jax.random.fold_in(own, 3), count)
    giver, receiver = mixed[0:count // 2 * 2:2], mixed[1:count // 2 * 2:2]
    slack = jnp.minimum(sizes[giver] - 1, reach - sizes[receiver]) // 2
    slack = jnp.where((giver == order[0]) | (receiver == order[0]) | (sizes[receiver] == 0), 0, jnp.maximum(slack, 0))
    shifted = jax.random.randint(jax.random.fold_in(own, 4), (count // 2,), 0, 1 << 20) % (slack + 1)
    sizes = sizes.at[giver].add(-shifted).at[receiver].add(shifted)
    items = jnp.searchsorted(jnp.cumsum(sizes), jnp.arange(rows * top), side="right").astype(jnp.int32)
    grid = items.reshape(top, rows).T
    grid = grid[jax.random.permutation(jax.random.fold_in(own, 1), rows)]
    offset_by = jax.random.randint(jax.random.fold_in(own, 2), (rows, 1), 0, top)
    return jnp.take_along_axis(grid, (jnp.arange(top)[None, :] + offset_by) % top, axis=1)


def portions_of(count, total, most, skew, full):
    weights = [(1 << 20) // math.isqrt(rank ** skew) + 1 for rank in range(1, count + 1)]
    largest = most if full else min(most, max(-(-total // count), total * weights[0] // sum(weights)))
    least = 1 if total - largest >= count - 1 else 0
    holding, rest = [largest] + [least] * (count - 1), total - largest - least * (count - 1)
    while rest > 0:
        free = [i for i in range(1, count) if holding[i] < largest] or [i for i in range(1, count) if holding[i] < most]
        pool, remaining = sum([weights[i] for i in free]), rest
        for i in free:
            more = min(most - holding[i], max(1, remaining * weights[i] // pool), rest)
            holding[i] = holding[i] + more
            rest = rest - more
    return np.array(holding)


def noise(key, shape, scale, bound, pieces=(), kind=jnp.bfloat16):
    values = scale * jax.random.normal(key, shape, jnp.float32)
    if pieces:
        values = values * block_levels(key, shape, pieces, -0.22, 0.18)
    return jnp.clip(values, -bound, bound).astype(kind)


def setup_inputs(seed: int = 0) -> dict:
    seeds = jax.random.split(jax.random.key(seed), 8)
    amplitudes = noise(seeds[0], (NOCC, NVIR, NVIR), 1.0, 6.0, ((0, 64), (2, 4)))
    orbitals = noise(seeds[1], (NAO, NVIR), NVIR ** -0.5, 0.375)
    tiles = noise(seeds[2], (TILE_SLOTS, NAO, NAO), (4 * NAO) ** -0.5, 0.125, ((0, 64), (2, 4)))
    tile_count = uneven(seeds[3], N_OCC, TILES, CAP, 2).astype(jnp.int32)
    tile_row = touch_ends(jax.random.randint(seeds[4], (TILE_SLOTS,), 0, ROWBLK), jax.random.fold_in(seeds[4], 1), 0, ROWBLK - 1).astype(jnp.int32)
    tile_src_keys = jax.random.split(jax.random.fold_in(seeds[5], 1), TILE_SLOTS // CAP)
    tile_src_turns = jax.random.permutation(jax.random.fold_in(seeds[5], 3), TILE_SLOTS // CAP)
    tile_src = jax.vmap(lambda own, number: routed_block(jax.random.fold_in(seeds[5], 2), own, number, CAP, N_OCC, 1, QMAX, 1))(tile_src_keys, tile_src_turns).reshape((TILE_SLOTS, 1))
    tile_sub = touch_ends(jax.random.randint(seeds[6], (TILE_SLOTS,), 0, ROWBLK), jax.random.fold_in(seeds[6], 1), 0, ROWBLK - 1).astype(jnp.int32)
    return {"amplitudes": amplitudes, "orbitals": orbitals, "tiles": tiles, "tile_count": tile_count, "tile_row": tile_row, "tile_src": tile_src, "tile_sub": tile_sub}


def reference(amplitudes, orbitals, tiles, tile_count, tile_row, tile_src, tile_sub):
    coeffs = orbitals.astype(jnp.float32)
    half_pairs = jnp.einsum('icd,nd->icn', amplitudes.astype(jnp.float32), coeffs).astype(jnp.bfloat16)
    pair_rows = jnp.einsum('mc,icn->imn', coeffs, half_pairs.astype(jnp.float32)).astype(jnp.bfloat16)
    pair_values = pair_rows.astype(jnp.float32)

    def add_tile(running, slot_id):
        owner = (slot_id // CAP).astype(jnp.int32)
        is_live = (slot_id % CAP) < tile_count[owner]
        row_block = (owner * ROWBLK + tile_row[slot_id]).astype(jnp.int32)
        col_block = (tile_src[slot_id, 0] * ROWBLK + tile_sub[slot_id]).astype(jnp.int32)

        def accumulate(current):
            column = lax.dynamic_slice_in_dim(pair_values, col_block, 1, 1)[:, 0, :]
            tile_f32 = lax.dynamic_index_in_dim(tiles, slot_id, 0, keepdims=False).astype(jnp.float32)
            term = jnp.dot(column, tile_f32.T, preferred_element_type=jnp.float32)
            before = lax.dynamic_slice_in_dim(current, row_block, 1, 1)
            return lax.dynamic_update_slice_in_dim(current, before + term[:, None, :], row_block, 1)

        def keep(current):
            return current

        return lax.cond(is_live, accumulate, keep, running), None

    start = jnp.zeros((NOCC, NAO, NAO), jnp.float32)
    ladder, _ = lax.scan(add_tile, start, jnp.arange(TILE_SLOTS, dtype=jnp.int32))
    ladder = ladder.astype(jnp.bfloat16)
    mixed = jnp.einsum('la,ils->ias', coeffs, ladder.astype(jnp.float32)).astype(jnp.bfloat16)
    sigma_out = jnp.einsum('ias,sb->iab', mixed.astype(jnp.float32), coeffs).astype(jnp.bfloat16)
    return sigma_out
```

```python
import jax
import jax.numpy as jnp
from jax import lax
from jax.experimental import pallas as pl
from jax.experimental.pallas import tpu as pltpu
from jax.sharding import PartitionSpec as P

BF16, F32 = jnp.bfloat16, jnp.float32


def ladder_kernel(count, rows, pairs, tile, orb, out, acc):
    slot = pl.program_id(0)

    @pl.when(slot == 0)
    def _():
        acc[...] = jnp.zeros_like(acc)

    @pl.when(slot < count[0])
    def _():
        folded = jnp.dot(orb[...], tile[0], preferred_element_type=F32).astype(BF16)
        term = lax.dot_general(
            pairs[0], folded, (((1,), (1,)), ((), ())), preferred_element_type=F32
        )
        acc[rows[slot]] += term

    @pl.when(slot == pl.num_programs(0) - 1)
    def _():
        out[...] = acc[...].astype(BF16)


def ladder_rows(count, rows, pairs, tiles, orb_t, blocks):
    slots, ao, part = tiles.shape
    occ = pairs.shape[1]
    vir = orb_t.shape[0]

    def live(t, c, r):
        return (jnp.minimum(t, c[0] - 1), 0, 0)

    return pl.pallas_call(
        ladder_kernel,
        out_shape=jax.ShapeDtypeStruct((blocks, occ, vir), BF16),
        grid_spec=pltpu.PrefetchScalarGridSpec(
            num_scalar_prefetch=2,
            grid=(slots,),
            in_specs=[
                pl.BlockSpec((1, occ, part), live),
                pl.BlockSpec((1, ao, part), live),
                pl.BlockSpec((vir, ao), lambda t, c, r: (0, 0)),
            ],
            out_specs=pl.BlockSpec((blocks, occ, vir), lambda t, c, r: (0, 0, 0)),
            scratch_shapes=[pltpu.VMEM((blocks, occ, vir), F32)],
        ),
        cost_estimate=pl.CostEstimate(
            flops=2 * slots * vir * part * (ao + occ),
            bytes_accessed=2 * slots * part * (ao + occ),
            transcendentals=0,
        ),
    )(count, rows, pairs, tiles, orb_t)


def shards(amplitudes, orbitals, tiles, tile_count, tile_row, tile_src, tile_sub):
    owners = lax.axis_size("occ")
    me = lax.axis_index("occ")
    quarter = lax.axis_index("ao")
    ao_count = orbitals.shape[0]
    ao_part = ao_count // lax.axis_size("ao")
    slots = tiles.shape[0]
    blocks = ao_count // owners
    nu_rows = lax.dynamic_slice_in_dim(orbitals, quarter * ao_part, ao_part, 0)
    amps = lax.all_gather(amplitudes, "ao", axis=2, tiled=True)
    half = jnp.einsum("icd,nd->icn", amps, nu_rows, preferred_element_type=F32).astype(BF16)
    half_all = lax.all_gather(half, "occ", axis=0, tiled=True)
    src = lax.dynamic_slice_in_dim(tile_src[:, 0], me * slots, slots, 0)
    sub = lax.dynamic_slice_in_dim(tile_sub, me * slots, slots, 0)
    row = lax.dynamic_slice_in_dim(tile_row, me * slots, slots, 0)
    count = lax.dynamic_slice_in_dim(tile_count, me, 1, 0)
    chosen = jnp.take(orbitals, src * blocks + sub, axis=0)
    pairs = jnp.einsum("tc,icn->tin", chosen, half_all, preferred_element_type=F32).astype(BF16)
    part = ladder_rows(count, row, pairs, tiles, orbitals.T, blocks)
    ladder = lax.psum_scatter(part, "ao", scatter_dimension=2, tiled=True)
    back = lax.all_to_all(ladder, "occ", split_axis=1, concat_axis=0, tiled=True)
    return jnp.einsum("la,lib->iab", orbitals, back, preferred_element_type=F32).astype(BF16)


def solution(mesh):
    placed = (P("occ", None, "ao"), P(), P("occ", None, "ao"), P(), P(), P(), P())
    return jax.shard_map(
        shards, mesh=mesh, in_specs=placed, out_specs=P("occ", None, "ao"), check_vma=False
    )
```

```python
import functools
import heapq
import itertools

import jax
import jax.numpy as jnp
from jax import lax
from jax.experimental import pallas as pl
from jax.experimental.pallas import tpu as pltpu
from jax.sharding import PartitionSpec as P

BF16, F32 = jnp.bfloat16, jnp.float32
MESH = pl.DeviceIdType.MESH
ZN, YN, XN = 8, 4, 4
NDEV = ZN * YN * 2
ROWS = 512
CUT = {"P": (0, 160, 304), "Q": (304, 416, 512)}
CLS = {"P": 0, "Q": 1}
ROW_ORDER = (0, 1, 7, 2, 6, 3, 5, 4)
SLOTS, NU, AO, VIR = 64, 128, 512, 256
USTEPS, PSTEPS, KSTEPS = 8, 4, 8
GSTEPS = PSTEPS + KSTEPS
GROUP = 32


def extent(cls, part):
    lo, mid, hi = CUT[cls]
    return {"f": (lo, hi - lo), "a": (lo, mid - lo), "b": (mid, hi - mid)}[part]


def route(rate=91e3, latency=1.7):
    free = {("z", 1): 0.0, ("z", -1): 0.0, ("y", 1): 0.0, ("y", -1): 0.0}
    tick = itertools.count()
    events, log, halves = [], [], {}

    def emit(now, cls, dz, dy, sends):
        for axis, way, part in sends:
            start = max(now, free[axis, way])
            free[axis, way] = start + 2 * 512 * extent(cls, part)[1] / rate
            at = ((dz - way) % ZN, dy) if axis == "z" else (dz, (dy - way) % YN)
            heapq.heappush(
                events, (free[axis, way] + latency, next(tick), cls, *at, part, axis, way)
            )

    for cls, axis in (("P", "z"), ("Q", "y"), ("P", "y"), ("Q", "z")):
        sends = [(axis, 1, "f"), (axis, -1, "f")]
        log.append((0.0, "own", cls, 0, 0, sends, axis == ("z" if cls == "P" else "y")))
        emit(0.0, cls, 0, 0, sends)
    while events:
        now, _, cls, dz, dy, part, axis, way = heapq.heappop(events)
        n = ZN if axis == "z" else YN
        gone = (-way * (dz if axis == "z" else dy)) % n
        sends = []
        if gone < n // 2 - 1:
            sends.append((axis, way, "f"))
        elif gone == n // 2 - 1:
            sends.append((axis, way, "a" if way == 1 else "b"))
        whole = part == "f"
        if not whole:
            seen = halves.setdefault((cls, dz, dy), set())
            seen.add(part)
            whole = len(seen) == 2
        if whole and axis == ("z" if cls == "P" else "y"):
            other = "y" if cls == "P" else "z"
            sends += [(other, 1, "f"), (other, -1, "f")]
        log.append((now, part, cls, dz, dy, sends, whole))
        emit(now, cls, dz, dy, sends)
    return log


def slots_of(log):
    table = [[] for _ in range(USTEPS + len(ROW_ORDER) * GSTEPS)]
    now, left = 0.0, list(range(len(log)))

    def take(step, test):
        nonlocal left
        table[step] += [e for e in left if test(log[e])]
        left = [e for e in left if not test(log[e])]

    for step in range(USTEPS):
        take(step, lambda e: e[0] <= now)
        now += 0.8
    for g, dz in enumerate(ROW_ORDER):
        ready = max(e[0] for e in log if e[3] == dz)
        for k in range(GSTEPS):
            step = USTEPS + g * GSTEPS + k
            if k == 0:
                now = max(now, ready)
            take(step, lambda e: e[0] <= now)
            now += 0.5 if k < PSTEPS else 0.3
    assert not left
    return table


def kernel(
    r2, w, csel, mask, orb_t, tiles, back,
    big, rg, tbuf, folded, prs, lhs, acc, sendbuf, recvbuf, outbuf,
    tsem, xsend, xrecv, isend, irecv, ssend, srecv, qsend, qrecv, asend, arecv,
):
    me = lax.axis_index("occ")
    q = lax.axis_index("ao")
    z, y, c = me // (2 * YN), (me // 2) % YN, me % 2
    log = route()
    table = slots_of(log)

    def dev(dz, dy, core):
        return (((z + dz + ZN) % ZN) * YN + (y + dy + YN) % YN) * 2 + core

    def occ(i):
        return {"occ": i}

    def ao(d):
        return {"ao": (q + d + XN) % XN}

    def remote(src, dst, ss, rs, to):
        return pltpu.make_async_remote_copy(
            src_ref=src, dst_ref=dst, send_sem=ss, recv_sem=rs, device_id=to, device_id_type=MESH
        )

    sibling = occ(dev(0, 0, 1 - c))

    def wait_recv(ref, sem):
        remote(ref, ref, sem, sem, sibling).wait_recv()

    def wait_send(ref, sem):
        remote(ref, ref, sem, sem, sibling).wait_send()

    load = pltpu.make_async_copy(tiles, tbuf, tsem)
    load.start()

    barrier = pltpu.get_barrier_semaphore()
    for d in range(1, XN):
        pl.semaphore_signal(barrier, inc=1, device_id=ao(d), device_id_type=MESH)

    def greet(d, carry):
        pl.semaphore_signal(
            barrier, inc=1, device_id=occ((me + d) % NDEV), device_id_type=MESH
        )
        return carry

    lax.fori_loop(1, NDEV, greet, 0)
    pl.semaphore_wait(barrier, XN - 1 + NDEV - 1)

    remote(r2, rg.at[3], xsend.at[0], xrecv.at[0], ao(1)).start()
    remote(r2, rg.at[1], xsend.at[1], xrecv.at[1], ao(-1)).start()
    wait_recv(rg.at[3], xrecv.at[0])
    remote(rg.at[3, 0], rg.at[2, 0], xsend.at[2], xrecv.at[2], ao(1)).start()
    wait_recv(rg.at[1], xrecv.at[1])
    remote(rg.at[1, 1], rg.at[2, 1], xsend.at[3], xrecv.at[3], ao(-1)).start()

    def term(block, k):
        return jnp.dot(block, w[k], preferred_element_type=F32)

    for j in range(2):
        part = term(r2[j], 0) + term(rg[3, j], 3) + term(rg[1, j], 1)
        wait_recv(rg.at[2, j], xrecv.at[2 + j])
        part = part + term(rg[2, j], 2)
        big[me, pl.ds(j * 256, 256), :] = part.astype(BF16)

    def piece(dz, dy, cls, part):
        return big.at[dev(dz, dy, c), pl.ds(*extent(cls, part))]

    def handle(event):
        _, part, cls, dz, dy, sends, whole = event
        if part != "own":
            wait_recv(
                piece(dz, dy, cls, part), irecv.at[CLS[cls], dz, dy, 1 if part == "b" else 0]
            )
        for axis, way, out in sends:
            to = occ(dev(way, 0, c) if axis == "z" else dev(0, way, c))
            at = ((dz - way) % ZN, dy) if axis == "z" else (dz, (dy - way) % YN)
            ref = piece(dz, dy, cls, out)
            remote(
                ref, ref, isend, irecv.at[CLS[cls], at[0], at[1], 1 if out == "b" else 0], to
            ).start()
        if whole:
            ref = piece(dz, dy, cls, "f")
            remote(ref, ref, ssend, srecv.at[dz, dy], sibling).start()

    def comm(step, lo, hi):
        if not any(table[lo:hi]):
            return
        if hi - lo == 1:
            for e in table[lo]:
                handle(log[e])
            return
        mid = (lo + hi) // 2

        @pl.when(step < mid)
        def _():
            comm(step, lo, mid)

        @pl.when(step >= mid)
        def _():
            comm(step, mid, hi)

    pairs = SLOTS // 2 // USTEPS

    def fold(step, carry):
        comm(step, 0, USTEPS)

        @pl.when(step == 0)
        def _():
            load.wait()

        for n in range(pairs):
            t = (step * pairs + n) * 2
            two = jnp.concatenate([tbuf[t], tbuf[t + 1]], axis=1)
            res = jnp.dot(orb_t[...], two, preferred_element_type=F32)
            folded[:, pl.ds(pl.multiple_of(t * NU, 256), 256)] = res.astype(BF16)
        return carry

    lax.fori_loop(0, USTEPS, fold, 0)

    row_in = lax.broadcasted_iota(jnp.int32, (GROUP, NU), 0) % 8 < 4
    left = lax.broadcasted_iota(jnp.int32, (GROUP, NU), 1) < 64

    def offset(g):
        return ((g + 1) // 2) * (2 * (g % 2) - 1)

    def finish(g):
        zrow = (z + offset(g) + ZN) % ZN
        wait_recv(recvbuf.at[g], qrecv.at[g])
        v = []
        for lp in range(4):
            total = sendbuf[g, q, lp].astype(F32)
            for k in range(XN - 1):
                total = total + recvbuf[g, k, lp].astype(F32)
            v.append(total)
        even = [
            jnp.where(row_in, v[0], pltpu.roll(v[1], 4, 0)),
            jnp.where(row_in, v[2], pltpu.roll(v[3], 4, 0)),
        ]
        odd = [
            jnp.where(row_in, pltpu.roll(v[0], GROUP - 4, 0), v[1]),
            jnp.where(row_in, pltpu.roll(v[2], GROUP - 4, 0), v[3]),
        ]
        for slot in range(8):
            k8 = slot // 2 * 8
            two = odd if slot % 2 else even
            rows = jnp.concatenate([two[0][k8 : k8 + 8], two[1][k8 : k8 + 8]], axis=0)
            outbuf[g, slot] = rows.astype(BF16)
        for slot in range(8):
            target = zrow * 8 + slot

            @pl.when(target != me)
            def _():
                remote(outbuf.at[g, slot], back.at[me], asend, arecv, occ(target)).start()

            @pl.when(target == me)
            def _():
                back[me] = outbuf[g, slot]

    def group(g, carry):
        dz = (offset(g) + ZN) % ZN
        zrow = (z + dz) % ZN

        def step(k, carry):
            comm(USTEPS + g * GSTEPS + k, USTEPS, len(table))

            @pl.when(k < PSTEPS)
            def _():
                yy = (y + k) % YN
                wait_recv(big.at[(zrow * YN + yy) * 2 + 1 - c], srecv.at[dz, k])
                for core in range(2):
                    slot = yy * 2 + core
                    for j in range(2):
                        res = jnp.dot(
                            csel[...],
                            big[zrow * 8 + slot, pl.ds(j * 256, 256), :],
                            preferred_element_type=F32,
                        )
                        for n in range(2):
                            at = (slot * 4 + 2 * j + n) * SLOTS
                            prs[pl.ds(pl.multiple_of(at, SLOTS), SLOTS), :] = res[
                                :, n * NU : (n + 1) * NU
                            ]

            @pl.when(k >= PSTEPS)
            def _():
                kc = k - PSTEPS
                cols = pl.multiple_of(kc * (8 * NU), 8 * NU)
                m = mask[:, pl.ds(cols, 8 * NU)]
                for t in range(8):
                    x = prs[pl.ds(kc * 8 + t, GROUP, stride=SLOTS), :]
                    for lam in range(8):
                        one = m[lam : lam + 1, t * NU : (t + 1) * NU]
                        lhs[pl.ds(lam * GROUP, GROUP), pl.ds(t * NU, NU)] = (x * one).astype(BF16)
                res = lax.dot_general(
                    lhs[...],
                    folded[:, pl.ds(cols, 8 * NU)],
                    (((1,), (1,)), ((), ())),
                    preferred_element_type=F32,
                )

                @pl.when(kc == 0)
                def _():
                    acc[...] = res

                @pl.when(kc > 0)
                def _():
                    acc[...] += res

            return carry

        lax.fori_loop(0, GSTEPS, step, 0)
        for lp in range(4):
            for h in range(2):
                cols = slice(h * NU, (h + 1) * NU)
                e = acc[pl.ds(2 * lp * GROUP, GROUP), cols]
                o = acc[pl.ds((2 * lp + 1) * GROUP, GROUP), cols]
                sendbuf[g, 2 * h, lp] = jnp.where(left, e, pltpu.roll(o, 64, 1)).astype(BF16)
                sendbuf[g, 2 * h + 1, lp] = jnp.where(left, pltpu.roll(e, 64, 1), o).astype(BF16)
        for k in range(1, XN):
            remote(
                sendbuf.at[g, (q + k) % XN], recvbuf.at[g, XN - 1 - k], qsend, qrecv.at[g], ao(k)
            ).start()

        @pl.when(g > 0)
        def _():
            finish(g - 1)

        return carry

    lax.fori_loop(0, ZN, group, 0)
    finish(ZN - 1)

    wait_send(r2, xsend.at[0])
    wait_send(r2, xsend.at[1])
    wait_send(rg.at[3, 0], xsend.at[2])
    wait_send(rg.at[1, 1], xsend.at[3])
    wait_send(big.at[pl.ds(0, 31)], isend)
    wait_send(big.at[pl.ds(0, 32)], ssend)
    wait_send(recvbuf, qsend)
    wait_send(back.at[pl.ds(0, NDEV - 1)], asend)
    wait_recv(back.at[pl.ds(0, NDEV - 1)], arecv)


def exchange(r2, w, csel, mask, orb_t, tiles):
    vmem = pl.BlockSpec(memory_space=pltpu.VMEM)
    dma = pltpu.SemaphoreType.DMA
    return pl.pallas_call(
        kernel,
        out_shape=jax.ShapeDtypeStruct((NDEV, 16, NU), BF16),
        in_specs=[vmem] * 5 + [pl.BlockSpec(memory_space=pl.ANY)],
        out_specs=vmem,
        scratch_shapes=[
            pltpu.VMEM((NDEV, ROWS, 256), BF16),
            pltpu.VMEM((XN, 2, VIR, NU), BF16),
            pltpu.VMEM((SLOTS, AO, NU), BF16),
            pltpu.VMEM((VIR, SLOTS * NU), BF16),
            pltpu.VMEM((GROUP * SLOTS, NU), F32),
            pltpu.VMEM((8 * GROUP, 8 * NU), BF16),
            pltpu.VMEM((8 * GROUP, VIR), F32),
            pltpu.VMEM((ZN, XN, 4, GROUP, NU), BF16),
            pltpu.VMEM((ZN, XN - 1, 4, GROUP, NU), BF16),
            pltpu.VMEM((ZN, 8, 16, NU), BF16),
            dma(()),
            dma((4,)),
            dma((4,)),
            dma(()),
            dma((2, ZN, YN, 2)),
            dma(()),
            dma((ZN, YN)),
            dma(()),
            dma((ZN,)),
            dma(()),
            dma(()),
        ],
        compiler_params=pltpu.CompilerParams(
            collective_id=0, has_side_effects=True, vmem_limit_bytes=56 * 2**20
        ),
    )(r2, w, csel, mask, orb_t, tiles)


def shards(amplitudes, orbitals, tiles, tile_count, tile_row, tile_src, tile_sub):
    me = lax.axis_index("occ")
    q = lax.axis_index("ao")
    blocks = AO // NDEV
    r2 = jnp.concatenate([amplitudes[0::2], amplitudes[1::2]], axis=2)
    mine = lax.dynamic_slice_in_dim(orbitals, q * NU, NU, 0)
    wt = jnp.roll(mine.T.reshape(XN, VIR // XN, NU), -q, axis=0)
    zero = jnp.zeros_like(wt)
    w = jnp.concatenate(
        [jnp.concatenate([wt, zero], axis=2), jnp.concatenate([zero, wt], axis=2)], axis=1
    )
    src = lax.dynamic_slice_in_dim(tile_src[:, 0], me * SLOTS, SLOTS, 0)
    sub = lax.dynamic_slice_in_dim(tile_sub, me * SLOTS, SLOTS, 0)
    row = lax.dynamic_slice_in_dim(tile_row, me * SLOTS, SLOTS, 0)
    live = jnp.arange(SLOTS, dtype=jnp.int32) < tile_count[me]
    csel = jnp.take(orbitals, src * blocks + sub, axis=0)
    picks = (row[None, :] == jnp.arange(blocks, dtype=jnp.int32)[:, None]) & live[None, :]
    mask = jnp.repeat(picks.astype(F32), NU, axis=1)
    back = exchange(r2, w, csel, mask, orbitals.T, tiles)
    back = back.reshape(NDEV, 4, 4, 2, 64)
    coef = orbitals.reshape(NDEV, 4, 2, VIR)
    return jnp.einsum("olpa,olipb->iab", coef, back, preferred_element_type=F32).astype(BF16)


def solution(mesh):
    placed = (P("occ", None, "ao"), P(), P("occ", None, "ao"), P(), P(), P(), P())
    return jax.shard_map(
        shards, mesh=mesh, in_specs=placed, out_specs=P("occ", None, "ao"), check_vma=False
    )
```

```python
import functools
import heapq
import itertools

import jax
import jax.numpy as jnp
from jax import lax
from jax.experimental import pallas as pl
from jax.experimental.pallas import tpu as pltpu
from jax.sharding import PartitionSpec as P

BF16, F32 = jnp.bfloat16, jnp.float32
MESH = pl.DeviceIdType.MESH
ZN, YN, XN = 8, 4, 4
NDEV = ZN * YN * 2
ROWS, WIDTH = 256, 512
CUT = {"P": (0, 80, 160), "Q": (160, 208, 256)}
CLS = {"P": 0, "Q": 1}
GROUPS = 8
ROW_ORDER = (0, 1, 7, 2, 6, 3, 5, 4)
SLOTS, NU, AO, VIR = 64, 128, 512, 256
USTEPS, PSTEPS, KSTEPS = 8, 4, 8
EARLY, EARLY2, FOLDS = 8, 16, 2
GSTEPS = PSTEPS + KSTEPS
GROUP = 32


def extent(cls, part):
    lo, mid, hi = CUT[cls]
    return {"f": (lo, hi - lo), "a": (lo, mid - lo), "b": (mid, hi - mid)}[part]


def route(rate=91e3, latency=1.7):
    free = {("z", 1): 0.0, ("z", -1): 0.0, ("y", 1): 0.0, ("y", -1): 0.0}
    tick = itertools.count()
    events, log, halves = [], [], {}

    def emit(now, cls, dz, dy, sends):
        for axis, way, part in sends:
            start = max(now, free[axis, way])
            free[axis, way] = start + 2 * 2 * WIDTH * extent(cls, part)[1] / rate
            at = ((dz - way) % ZN, dy) if axis == "z" else (dz, (dy - way) % YN)
            heapq.heappush(
                events, (free[axis, way] + latency, next(tick), cls, *at, part, axis, way)
            )

    for cls, axis in (("P", "z"), ("Q", "y"), ("P", "y"), ("Q", "z")):
        sends = [(axis, 1, "f"), (axis, -1, "f")]
        log.append((0.0, "own", cls, 0, 0, sends, axis == ("z" if cls == "P" else "y")))
        emit(0.0, cls, 0, 0, sends)
    while events:
        now, _, cls, dz, dy, part, axis, way = heapq.heappop(events)
        n = ZN if axis == "z" else YN
        gone = (-way * (dz if axis == "z" else dy)) % n
        sends = []
        if gone < n // 2 - 1:
            sends.append((axis, way, "f"))
        elif gone == n // 2 - 1:
            sends.append((axis, way, "a" if way == 1 else "b"))
        whole = part == "f"
        if not whole:
            seen = halves.setdefault((cls, dz, dy), set())
            seen.add(part)
            whole = len(seen) == 2
        if whole and axis == ("z" if cls == "P" else "y"):
            other = "y" if cls == "P" else "z"
            sends += [(other, 1, "f"), (other, -1, "f")]
        log.append((now, part, cls, dz, dy, sends, whole))
        emit(now, cls, dz, dy, sends)
    return log


def order_of(log):
    whole = {}
    for now, _, _, dz, dy, _, _ in log:
        whole[dz * YN + dy] = max(now, whole.get(dz * YN + dy, 0.0))
    return [dz * YN + dy for dz in ROW_ORDER for dy in range(YN)], whole


def slots_of(log):
    table = [[] for _ in range(USTEPS + GROUPS * GSTEPS)]
    order, whole = order_of(log)
    now, left = 0.0, list(range(len(log)))

    def take(step, test):
        nonlocal left
        table[step] += [e for e in left if test(log[e])]
        left = [e for e in left if not test(log[e])]

    for step in range(USTEPS):
        take(step, lambda e: e[0] <= now)
        now += 0.8
    for g in range(GROUPS):
        for k in range(GSTEPS):
            if k < PSTEPS:
                now = max(now, whole[order[g * 4 + k]])
            take(USTEPS + g * GSTEPS + k, lambda e: e[0] <= now)
            now += 0.5 if k < PSTEPS else 0.3
    assert not left
    return table


def kernel(
    amps, orb, src, sub, row, count, tiles, back,
    big, rg, tbuf, folded, prs, acc, sendbuf, recvbuf, outbuf, orb_t, csel, pick,
    tsem, xsend, xrecv, isend, irecv, ssend, srecv, qsend, qrecv, asend, arecv,
):
    me = lax.axis_index("occ")
    q = lax.axis_index("ao")
    z, y, c = me // (2 * YN), (me // 2) % YN, me % 2
    log = route()
    table = slots_of(log)

    def dev(dz, dy, core):
        return (((z + dz + ZN) % ZN) * YN + (y + dy + YN) % YN) * 2 + core

    def occ(i):
        return {"occ": i}

    def ao(d):
        return {"ao": (q + d + XN) % XN}

    def remote(src, dst, ss, rs, to):
        return pltpu.make_async_remote_copy(
            src_ref=src, dst_ref=dst, send_sem=ss, recv_sem=rs, device_id=to, device_id_type=MESH
        )

    sibling = occ(dev(0, 0, 1 - c))

    def wait_recv(ref, sem):
        remote(ref, ref, sem, sem, sibling).wait_recv()

    def wait_send(ref, sem):
        remote(ref, ref, sem, sem, sibling).wait_send()

    load = pltpu.make_async_copy(tiles, tbuf, tsem)
    load.start()

    barrier = pltpu.get_barrier_semaphore()
    for d in range(1, XN):
        pl.semaphore_signal(barrier, inc=1, device_id=ao(d), device_id_type=MESH)

    def greet(d, carry):
        pl.semaphore_signal(
            barrier, inc=1, device_id=occ((me + d) % NDEV), device_id_type=MESH
        )
        return carry

    lax.fori_loop(1, NDEV, greet, 0)

    orb_t[...] = orb[...].astype(F32).T.astype(BF16)

    def own_slots(ref):
        v = ref[pl.ds(me // 2, 1), :].astype(F32)
        return jnp.where(c == 1, pltpu.roll(v, 64, 1), v)

    block = own_slots(src) * 8.0 + own_slots(sub)
    block = jnp.broadcast_to(block, (128, 128)).T[:SLOTS]
    lane = lax.broadcasted_iota(jnp.int32, (SLOTS, 128), 1).astype(F32)
    chosen = jnp.concatenate(
        [(block == lane + 128.0 * n).astype(F32).astype(BF16) for n in range(4)], axis=1
    )
    csel[...] = jnp.dot(chosen, orb[...], preferred_element_type=F32).astype(BF16)

    def choose(t, carry):
        r = jnp.where(t < count[me], row[me // 2, c * SLOTS + t], 8)
        for lam in range(8):
            pick[lam, t] = jnp.where(r == lam, 1.0, 0.0)
        return carry

    lax.fori_loop(0, SLOTS, choose, 0)
    pl.semaphore_wait(barrier, XN - 1 + NDEV - 1)

    def quarter(d, lo, n):
        return rg.at[(q + d + XN) % XN, pl.ds(lo, n)]

    front, rear = pl.ds(0, 2), pl.ds(2, 2)
    remote(amps.at[front], quarter(0, 0, 2), xsend.at[0], xrecv.at[0], ao(1)).start()
    remote(amps.at[rear], quarter(0, 2, 2), xsend.at[1], xrecv.at[1], ao(-1)).start()
    remote(amps.at[rear], quarter(0, 2, 2), xsend.at[4], xrecv.at[4], ao(1)).start()
    remote(amps.at[front], quarter(0, 0, 2), xsend.at[5], xrecv.at[5], ao(-1)).start()
    rg[q] = amps[...]

    load.wait()

    def fold(step, carry):
        t = step * 2
        two = jnp.concatenate([tbuf[t], tbuf[t + 1]], axis=1)
        res = jnp.dot(orb_t[...], two, preferred_element_type=F32)
        folded[pl.ds(pl.multiple_of(t * NU, 256), 256), :] = res.T.astype(BF16)
        return carry

    lax.fori_loop(0, EARLY, fold, 0)

    wait_recv(quarter(-1, 0, 2), xrecv.at[0])
    remote(quarter(-1, 0, 2), quarter(-1, 0, 2), xsend.at[2], xrecv.at[2], ao(1)).start()
    wait_recv(quarter(1, 2, 2), xrecv.at[1])
    remote(quarter(1, 2, 2), quarter(1, 2, 2), xsend.at[3], xrecv.at[3], ao(-1)).start()
    lax.fori_loop(EARLY, EARLY2, fold, 0)
    mine = orb[pl.ds(pl.multiple_of(q * NU, NU), NU), :]
    wait_recv(quarter(-1, 2, 2), xrecv.at[4])
    wait_recv(quarter(1, 0, 2), xrecv.at[5])
    for j in range(2):
        wait_recv(quarter(2, 2 * j, 2), xrecv.at[2 + j])
        for i in (2 * j, 2 * j + 1):
            whole = jnp.concatenate([rg[k, i] for k in range(XN)], axis=0)
            part = jnp.dot(mine, whole, preferred_element_type=F32)
            big[me, :, pl.ds(i * NU, NU)] = part.T.astype(BF16)

    def piece(dz, dy, cls, part):
        return big.at[dev(dz, dy, c), pl.ds(*extent(cls, part))]

    def handle(event):
        _, part, cls, dz, dy, sends, whole = event
        if part != "own":
            wait_recv(
                piece(dz, dy, cls, part), irecv.at[CLS[cls], dz, dy, 1 if part == "b" else 0]
            )
        for axis, way, out in sends:
            to = occ(dev(way, 0, c) if axis == "z" else dev(0, way, c))
            at = ((dz - way) % ZN, dy) if axis == "z" else (dz, (dy - way) % YN)
            ref = piece(dz, dy, cls, out)
            remote(
                ref, ref, isend, irecv.at[CLS[cls], at[0], at[1], 1 if out == "b" else 0], to
            ).start()
        if whole:
            ref = piece(dz, dy, cls, "f")
            remote(ref, ref, ssend, srecv.at[dz, dy], sibling).start()

    def comm(step, lo, hi):
        if not any(table[lo:hi]):
            return
        if hi - lo == 1:
            for e in table[lo]:
                handle(log[e])
            return
        mid = (lo + hi) // 2

        @pl.when(step < mid)
        def _():
            comm(step, lo, mid)

        @pl.when(step >= mid)
        def _():
            comm(step, mid, hi)

    def fold_rest(step, carry):
        comm(step, 0, USTEPS)
        lax.fori_loop(EARLY2 + step * FOLDS, EARLY2 + (step + 1) * FOLDS, fold, 0)
        return carry

    lax.fori_loop(0, USTEPS, fold_rest, 0)

    row_in = lax.broadcasted_iota(jnp.int32, (GROUP, NU), 0) % 8 < 4
    left = lax.broadcasted_iota(jnp.int32, (GROUP, NU), 1) < 64

    def offset(g):
        return (((g + 1) // 2) * (2 * (g % 2) - 1) + ZN) % ZN

    def finish(g):
        wait_recv(recvbuf.at[g], qrecv.at[g])
        v = []
        for lp in range(4):
            total = sendbuf[g, q, lp].astype(F32)
            for k in range(XN - 1):
                total = total + recvbuf[g, k, lp].astype(F32)
            v.append(total)
        even = [
            jnp.where(row_in, v[0], pltpu.roll(v[1], 4, 0)),
            jnp.where(row_in, v[2], pltpu.roll(v[3], 4, 0)),
        ]
        odd = [
            jnp.where(row_in, pltpu.roll(v[0], GROUP - 4, 0), v[1]),
            jnp.where(row_in, pltpu.roll(v[2], GROUP - 4, 0), v[3]),
        ]
        for slot in range(8):
            k8 = slot // 2 * 8
            two = odd if slot % 2 else even
            rows = jnp.concatenate([two[0][k8 : k8 + 8], two[1][k8 : k8 + 8]], axis=0)
            outbuf[g, slot] = rows.astype(BF16)
        dz = offset(g)
        for slot in range(8):
            target = dev(dz, slot // 2, slot % 2)

            @pl.when(target != me)
            def _():
                remote(outbuf.at[g, slot], back.at[me], asend, arecv, occ(target)).start()

            @pl.when(target == me)
            def _():
                back[me] = outbuf[g, slot]

    def group(g, carry):
        dz = offset(g)

        def step(k, carry):
            comm(USTEPS + g * GSTEPS + k, USTEPS, len(table))

            @pl.when(k < PSTEPS)
            def _():
                dy = k
                wait_recv(big.at[dev(dz, dy, 1 - c)], srecv.at[dz, dy])
                for core in range(2):
                    slot = k * 2 + core
                    res = jnp.dot(
                        csel[...], big[dev(dz, dy, core)], preferred_element_type=F32
                    )
                    for n in range(4):
                        at = (slot * 4 + n) * SLOTS
                        prs[pl.ds(pl.multiple_of(at, SLOTS), SLOTS), :] = res[
                            :, n * NU : (n + 1) * NU
                        ]

            @pl.when(k >= PSTEPS)
            def _():
                kc = k - PSTEPS
                outs = []
                for n in range(8):
                    t = kc * 8 + n
                    x = prs[pl.ds(t, GROUP, stride=SLOTS), :].astype(BF16)
                    rows = folded[pl.ds(pl.multiple_of(t * NU, NU), NU), :]
                    outs.append(jnp.dot(x, rows, preferred_element_type=F32))
                for lam in range(8):
                    total = outs[0] * pick[lam, kc * 8]
                    for n in range(1, 8):
                        total = total + outs[n] * pick[lam, kc * 8 + n]
                    acc[lam] += total

            return carry

        acc[...] = jnp.zeros_like(acc)
        lax.fori_loop(0, GSTEPS, step, 0)
        for lp in range(4):
            for h in range(2):
                cols = slice(h * NU, (h + 1) * NU)
                e = acc[2 * lp, :, cols]
                o = acc[2 * lp + 1, :, cols]
                sendbuf[g, 2 * h, lp] = jnp.where(left, e, pltpu.roll(o, 64, 1)).astype(BF16)
                sendbuf[g, 2 * h + 1, lp] = jnp.where(left, pltpu.roll(e, 64, 1), o).astype(BF16)
        for k in range(1, XN):
            remote(
                sendbuf.at[g, (q + k) % XN], recvbuf.at[g, XN - 1 - k], qsend, qrecv.at[g], ao(k)
            ).start()

        @pl.when(g > 0)
        def _():
            finish(g - 1)

        return carry

    lax.fori_loop(0, GROUPS, group, 0)
    finish(GROUPS - 1)

    for n in (0, 1, 4, 5):
        wait_send(amps.at[front], xsend.at[n])
    wait_send(quarter(-1, 0, 2), xsend.at[2])
    wait_send(quarter(1, 2, 2), xsend.at[3])
    wait_send(big.at[pl.ds(0, 31)], isend)
    wait_send(big.at[pl.ds(0, 32)], ssend)
    wait_send(recvbuf, qsend)
    wait_send(back.at[pl.ds(0, NDEV - 1)], asend)
    wait_recv(back.at[pl.ds(0, NDEV - 1)], arecv)


def exchange(amps, orb, src, sub, row, count, tiles):
    vmem = pl.BlockSpec(memory_space=pltpu.VMEM)
    dma = pltpu.SemaphoreType.DMA
    return pl.pallas_call(
        kernel,
        out_shape=jax.ShapeDtypeStruct((NDEV, 16, NU), BF16),
        in_specs=[vmem] * 4
        + [pl.BlockSpec(memory_space=pltpu.SMEM)] * 2
        + [pl.BlockSpec(memory_space=pl.ANY)],
        out_specs=vmem,
        scratch_shapes=[
            pltpu.VMEM((NDEV, ROWS, WIDTH), BF16),
            pltpu.VMEM((XN, 4, VIR // XN, VIR), BF16),
            pltpu.VMEM((SLOTS, AO, NU), BF16),
            pltpu.VMEM((SLOTS * NU, VIR), BF16),
            pltpu.VMEM((GROUP * SLOTS, NU), F32),
            pltpu.VMEM((8, GROUP, VIR), F32),
            pltpu.VMEM((ZN, XN, 4, GROUP, NU), BF16),
            pltpu.VMEM((ZN, XN - 1, 4, GROUP, NU), BF16),
            pltpu.VMEM((ZN, 8, 16, NU), BF16),
            pltpu.VMEM((VIR, AO), BF16),
            pltpu.VMEM((SLOTS, VIR), BF16),
            pltpu.SMEM((8, SLOTS), F32),
            dma(()),
            dma((6,)),
            dma((6,)),
            dma(()),
            dma((2, ZN, YN, 2)),
            dma(()),
            dma((ZN, YN)),
            dma(()),
            dma((ZN,)),
            dma(()),
            dma(()),
        ],
        compiler_params=pltpu.CompilerParams(
            collective_id=0, has_side_effects=True, vmem_limit_bytes=56 * 2**20
        ),
    )(amps, orb, src, sub, row, count, tiles)


def shards(amplitudes, orbitals, tiles, tile_count, tile_row, tile_src, tile_sub):
    back = exchange(
        amplitudes.transpose(0, 2, 1),
        orbitals,
        tile_src.reshape(32, 128),
        tile_sub.reshape(32, 128),
        tile_row.reshape(32, 128),
        tile_count,
        tiles,
    )
    back = back.reshape(NDEV, 4, 4, 2, 64)
    coef = orbitals.reshape(NDEV, 4, 2, VIR)
    return jnp.einsum("olpa,olipb->iab", coef, back, preferred_element_type=F32).astype(BF16)


def solution(mesh):
    placed = (P("occ", None, "ao"), P(), P("occ", None, "ao"), P(), P(), P(), P())
    return jax.shard_map(
        shards, mesh=mesh, in_specs=placed, out_specs=P("occ", None, "ao"), check_vma=False
    )
```
